32 devices in a mesh: groups: 2 (over y), fld: 8 (over z, x), rep: 2 (over core).
Axes of the slice: x: 2, y: 2, z: 4, core: 2. Of those that a mesh axis runs over, the one named last changes fastest.
Arguments:
- feature_ids: int32 [4096, 40], P('groups', 'fld'), parts along dimension 0, may hold values from 0 to 65535, as said below
- field_slot: int32 [40], replicated, may hold values from 0 to 39, as said below
- table: bfloat16 [2621440, 64], P(('fld', 'rep')), may hold values from -48 to 48
- query_weight: bfloat16 [2, 64, 64], replicated, may hold values from -0.75 to 0.75
- key_weight: bfloat16 [2, 64, 64], replicated, may hold values from -0.75 to 0.75
- value_weight: bfloat16 [2, 64, 64], replicated, may hold values from -0.75 to 0.75
- residual_weight: bfloat16 [2, 64, 64], replicated, may hold values from -0.75 to 0.75
- out_weight: float32 [40, 64], replicated, may hold values from -0.125 to 0.125
Outputs:
- interacted: bfloat16 [40, 4096, 64], P('fld', ('groups', 'rep')), parts along dimension 1
- logits: float32 [2, 2048], P('rep', ('groups', 'fld')), parts along dimension 1
The draws below stay inside these ranges and needn't reach their ends.
There are 2 independent parts, one for each index of `groups`. The reference program is written for one: setup_inputs(seed, part) draws one part's arguments, and reference() takes and returns one part's arrays. A program takes and returns all parts, laid end to end along the dimension named above; an argument that names none is the same for every part. Nothing has to cross between parts.
Inputs may be any that keep to these rules, and one draw needn't show every extreme that they name: `feature_ids`: in each column the ids lie below a table size of that slot, which differs from slot to slot. `field_slot`: distinct slots.
All inputs are finite; a program needn't handle non-finite values.
Results may differ from the reference program's by a relative error of at most 0.006.
The reference program's roundings to bfloat16 on the way count: a program that leaves them out, or rounds other values in their place, can miss the bound.
Values may be sent and summed in bfloat16 or wider, within the bound.
A program may use at most 128 MiB of HBM per device.

```python
import jax
import jax.numpy as jnp
from jax import lax

FEATURE_FIELDS = 40
WIDTH = 64
HEADS = 2
ROWS_SLOT = 65536
LAYERS = 2
EX_DEV = 128
SLOTS = 40
EXAMPLES = 2048
N_REP = 2


def draw_feature_ids(key, part):
    size_key = jax.random.fold_in(key, 11)
    id_key = jax.random.fold_in(key, 12)
    table_sizes = jax.random.randint(size_key, (1, SLOTS), ROWS_SLOT // 8, ROWS_SLOT + 1)
    return jax.random.randint(id_key, (EXAMPLES, SLOTS), 0, table_sizes).astype(jnp.int32)


def draw_field_slot(key, part):
    order_key = jax.random.fold_in(key, 31)
    return jax.random.permutation(order_key, SLOTS)[:FEATURE_FIELDS].astype(jnp.int32)


def draw_table(key, part):
    normal_values = jax.random.normal(jax.random.fold_in(key, 21), (SLOTS * ROWS_SLOT, WIDTH), jnp.float32)
    return jnp.clip(normal_values, -4.0, 4.0).astype(jnp.bfloat16)


def bell_draw(key, shape, deviation, reach, kind=jnp.bfloat16):
    entries = jax.random.normal(key, shape, jnp.float32) * deviation
    return jnp.minimum(jnp.maximum(entries, -reach), reach).astype(kind)


def setup_inputs(seed: int = 0, part: int = 0) -> dict:
    key_of = jax.random.split(jax.random.key(seed), 9)
    own_keys = jax.random.split(jax.random.fold_in(key_of[8], part), 9)
    feature_ids = draw_feature_ids(jax.random.fold_in(jax.random.fold_in(key_of[8], part), 71), part)
    field_slot = draw_field_slot(jax.random.fold_in(key_of[8], 71), part)
    table = draw_table(jax.random.fold_in(key_of[8], 71), part)
    query_weight = bell_draw(key_of[3], (LAYERS, WIDTH, WIDTH), WIDTH ** -0.5, 0.75)
    key_weight = bell_draw(key_of[4], (LAYERS, WIDTH, WIDTH), WIDTH ** -0.5, 0.75)
    value_weight = bell_draw(key_of[5], (LAYERS, WIDTH, WIDTH), WIDTH ** -0.5, 0.75)
    residual_weight = bell_draw(key_of[6], (LAYERS, WIDTH, WIDTH), WIDTH ** -0.5, 0.75)
    out_weight = bell_draw(key_of[7], (FEATURE_FIELDS, WIDTH), (FEATURE_FIELDS * WIDTH) ** -0.5, 0.125, jnp.float32)
    return dict(feature_ids=feature_ids, field_slot=field_slot, table=table, query_weight=query_weight, key_weight=key_weight, value_weight=value_weight, residual_weight=residual_weight, out_weight=out_weight)


def rounded(values):
    return lax.optimization_barrier(values.astype(jnp.bfloat16)).astype(jnp.float32)

def attend(layer_in, w_query, w_key, w_value, w_skip, head_count):
    batch_rows, field_count, width = layer_in.shape
    head_size = width // head_count
    source = layer_in.astype(jnp.float32)

    def project(weight):
        return jnp.einsum('nfe,ed->nfd', source, weight.astype(jnp.float32))
    query_rows = rounded(project(w_query)).reshape(batch_rows, field_count, head_count, head_size)
    matches = rounded(project(w_key)).reshape(batch_rows, field_count, head_count, head_size)
    contents = rounded(project(w_value)).reshape(batch_rows, field_count, head_count, head_size)
    skip_output = project(w_skip)
    scores = jnp.einsum('nfhd,nghd->nhfg', query_rows, matches) / jnp.sqrt(jnp.float32(head_size))
    attention = rounded(jax.nn.softmax(scores, axis=-1))
    mixed = jnp.einsum('nhfg,nghd->nfhd', attention, contents).reshape(batch_rows, field_count, width)
    return jax.nn.relu(mixed + skip_output).astype(jnp.bfloat16)

def reference(feature_ids, field_slot, table, query_weight, key_weight, value_weight, residual_weight, out_weight):
    slot_range = jnp.arange(SLOTS, dtype=jnp.int32)
    select_mask = (field_slot[:, None] == slot_range[None, :]).astype(jnp.float32)
    blocks = feature_ids.reshape(EXAMPLES // EX_DEV, EX_DEV, SLOTS)

    def one_block(block_ids):
        row_index = block_ids + (slot_range * ROWS_SLOT)[None, :]
        looked = jnp.take(table, row_index, axis=0).astype(jnp.float32)
        layer_in = jnp.einsum('nse,fs->nfe', looked, select_mask).astype(jnp.bfloat16)
        for layer in range(LAYERS):
            layer_in = attend(layer_in, query_weight[layer], key_weight[layer], value_weight[layer], residual_weight[layer], HEADS)
        hidden_state = layer_in.astype(jnp.float32)
        logit_rows = jnp.einsum('nfd,fd->n', hidden_state, out_weight, precision=lax.Precision.HIGHEST)
        placed = jnp.einsum('nfd,fs->snd', hidden_state, select_mask).astype(jnp.bfloat16)
        return (placed, logit_rows)
    placed, logit_rows = lax.map(one_block, blocks)
    interacted = jnp.transpose(placed, (1, 0, 2, 3)).reshape(SLOTS, EXAMPLES, WIDTH)
    logits = logit_rows.reshape(N_REP, EXAMPLES // N_REP)
    return (interacted, logits)
```

```python
import functools
import math

import jax
import jax.numpy as jnp
from jax import lax
from jax.experimental import pallas as pl
from jax.experimental.pallas import tpu as pltpu
from jax.sharding import PartitionSpec as P

HEADS = 2
f32, bf16 = jnp.float32, jnp.bfloat16

def interact_body(layers, heads, x, wt, ow, out, logit, xs, q, k, v, skip, qt, att, mt):
    fields, width, lanes = x.shape
    size = width // heads
    scale = 1.0 / math.sqrt(size)
    gb, db = 4, 4

    def layer_step(l, source):
        def project(f, carry):
            p = jnp.dot(wt[l], source[f], preferred_element_type=f32)
            base = pl.multiple_of(f * width, width)
            q[pl.ds(base, width), :] = p[0:width].astype(bf16).astype(f32)
            k[pl.ds(base, width), :] = p[width:2 * width].astype(bf16).astype(f32)
            v[pl.ds(base, width), :] = p[2 * width:3 * width].astype(bf16).astype(f32)
            skip[pl.ds(base, width), :] = p[3 * width:4 * width]
            return carry
        lax.fori_loop(0, fields, project, 0, unroll=4)

        def turn(d, carry):
            qt[pl.ds(pl.multiple_of(d * fields, 8), fields), :] = q[pl.ds(d, fields, stride=width), :] * scale
            return carry
        lax.fori_loop(0, width, turn, 0, unroll=8)

        for h in range(heads):
            def match(gi, top):
                acc = [jnp.zeros((fields, lanes), f32) for _ in range(gb)]
                for d in range(h * size, (h + 1) * size):
                    qd = qt[d * fields:(d + 1) * fields, :]
                    for j in range(gb):
                        row = k[pl.ds((gi * gb + j) * width + d, 1), :]
                        acc[j] = acc[j] + qd * row
                for j in range(gb):
                    att[h, gi * gb + j] = acc[j]
                    top = jnp.maximum(top, acc[j])
                return top
            top = lax.fori_loop(0, fields // gb, match, jnp.full((fields, lanes), -jnp.inf, f32))

            def expo(g, total):
                e = jnp.exp(att[h, g] - top)
                att[h, g] = e
                return total + e
            total = lax.fori_loop(0, fields, expo, jnp.zeros((fields, lanes), f32), unroll=4)
            inverse = 1.0 / total

            def norm(g, carry):
                att[h, g] = (att[h, g] * inverse).astype(bf16).astype(f32)
                return carry
            lax.fori_loop(0, fields, norm, 0, unroll=4)

        def mix(di, carry):
            h = di // (size // db)
            acc = [jnp.zeros((fields, lanes), f32) for _ in range(db)]
            for g in range(fields):
                a = att[h, g]
                for j in range(db):
                    row = v[pl.ds(g * width + di * db + j, 1), :]
                    acc[j] = acc[j] + a * row
            for j in range(db):
                mt[pl.ds(pl.multiple_of((di * db + j) * fields, 8), fields), :] = acc[j]
            return carry
        lax.fori_loop(0, width // db, mix, 0)

    def finish(f):
        m = mt[pl.ds(f, width, stride=fields), :]
        s = skip[pl.ds(pl.multiple_of(f * width, width), width), :]
        return jnp.maximum(m + s, 0.0).astype(bf16)

    for l in range(layers):
        layer_step(l, x if l == 0 else xs)
        if l < layers - 1:
            def close(f, carry):
                xs[f] = finish(f)
                return carry
            lax.fori_loop(0, fields, close, 0, unroll=4)
        else:
            total = jnp.zeros((width, lanes), f32)
            for f in range(fields):
                hid = finish(f)
                out[f] = hid
                total = total + hid.astype(f32) * ow[:, f:f + 1]
            logit[...] = jnp.sum(total, axis=0, keepdims=True)

def interact(x, wt, ow):
    fields, width, lanes = x.shape
    layers = wt.shape[0]
    flat = pltpu.VMEM((fields * width, lanes), f32)
    return pl.pallas_call(
        functools.partial(interact_body, layers, HEADS),
        out_shape=(jax.ShapeDtypeStruct(x.shape, bf16), jax.ShapeDtypeStruct((1, lanes), f32)),
        in_specs=[pl.BlockSpec(memory_space=pltpu.VMEM)] * 3,
        out_specs=(pl.BlockSpec(memory_space=pltpu.VMEM),) * 2,
        scratch_shapes=[pltpu.VMEM(x.shape, bf16), flat, flat, flat, flat, flat,
                        pltpu.VMEM((HEADS, fields, fields, lanes), f32), flat],
        compiler_params=pltpu.CompilerParams(vmem_limit_bytes=40 << 20),
    )(x, wt, ow)


def lookup_body(ready, rows, valid, table, out, held, sems):
    tiles, slots, width, lanes = out.shape
    piece = table.shape[1] // sems.shape[0]
    copies = [
        pltpu.make_async_copy(
            table.at[:, c * piece:(c + 1) * piece], held.at[:, c * piece:(c + 1) * piece], sems.at[c]
        )
        for c in range(sems.shape[0])
    ]
    for copy in copies:
        copy.start()
    lane = lax.broadcasted_iota(jnp.int32, (1, lanes), 1)
    done = 0
    for j in range(slots):
        while done < len(copies) and done * piece < ready[j]:
            copies[done].wait()
            done += 1

        def tile(t, carry):
            acc = jnp.zeros((width, lanes), bf16)
            for i in range(lanes):
                row = rows[j, t * lanes + i]
                start = pl.multiple_of((row >> 7) * 128, 128)
                block = pltpu.roll(held[:, pl.ds(start, lanes)], (i - row) & 127, 1)
                acc = jnp.where(lane == i, block, acc)
            keep = valid[j, pl.ds(t, 1), :] > 0
            out[t, j] = jnp.where(keep, acc, jnp.zeros_like(acc))
            return carry
        lax.fori_loop(0, tiles, tile, 0)
    for copy in copies[done:]:
        copy.wait()


def pieces(owned):
    return next(c for c in (5, 4, 3, 2, 1) if owned % (c * 128) == 0)


def lookup(rows, valid, table_t, ready):
    slots, tiles, lanes = valid.shape
    width, owned = table_t.shape
    return pl.pallas_call(
        functools.partial(lookup_body, ready),
        out_shape=jax.ShapeDtypeStruct((tiles, slots, width, lanes), bf16),
        in_specs=[
            pl.BlockSpec(memory_space=pltpu.SMEM),
            pl.BlockSpec(memory_space=pltpu.VMEM),
            pl.BlockSpec(memory_space=pl.ANY),
        ],
        out_specs=pl.BlockSpec(memory_space=pltpu.VMEM),
        scratch_shapes=[
            pltpu.VMEM((width, owned), bf16),
            pltpu.SemaphoreType.DMA((pieces(owned),)),
        ],
        compiler_params=pltpu.CompilerParams(vmem_limit_bytes=48 << 20),
    )(rows, valid, table_t)


def per_device(
    feature_ids, field_slot, table, query_weight, key_weight, value_weight, residual_weight, out_weight
):
    examples, slots = feature_ids.shape
    owned, width = table.shape
    fld = lax.axis_size("fld")
    rep = lax.axis_size("rep")
    me = lax.axis_index("rep")
    rows_slot = owned * rep // slots
    lanes = examples // rep // fld
    firsts = [r * owned // rows_slot for r in range(rep)]
    lasts = [-(-(r + 1) * owned // rows_slot) for r in range(rep)]
    near = max(b - a for a, b in zip(firsts, lasts))
    firsts = [min(a, slots - near) for a in firsts]
    ready = [
        max(min(owned, (a + j + 1) * rows_slot - r * owned) for r, a in enumerate(firsts))
        for j in range(near)
    ]
    first = sum((me == r) * a for r, a in enumerate(firsts)).astype(jnp.int32)
    near_ids = lax.dynamic_slice_in_dim(jnp.transpose(feature_ids), first, near, 0)
    offset = (first + jnp.arange(near, dtype=jnp.int32)) * rows_slot - me * owned
    rows = near_ids + offset[:, None]
    valid = ((rows >= 0) & (rows < owned)).astype(jnp.int32)
    rows = jnp.clip(rows, 0, owned - 1)
    found = lookup(rows, valid.reshape(near, -1, lanes), jnp.transpose(table), ready)
    found = found.reshape(rep, fld, near, width, lanes)
    own = lax.dynamic_index_in_dim(found, me, 0, False)
    looked = jnp.zeros((fld, slots, width, lanes), bf16)
    looked = lax.dynamic_update_slice_in_dim(looked, own, first, 1)
    for step in range(1, rep):
        route = [(r, (r + step) % rep) for r in range(rep)]
        got = lax.ppermute(lax.dynamic_index_in_dim(found, (me + step) % rep, 0, False), "rep", route)
        source = (me - step) % rep
        start = sum((source == r) * a for r, a in enumerate(firsts)).astype(jnp.int32)
        old = lax.dynamic_slice_in_dim(looked, start, near, 1)
        looked = lax.dynamic_update_slice_in_dim(looked, old + got, start, 1)
    arrived = lax.all_to_all(looked, "fld", split_axis=0, concat_axis=0, tiled=True)
    layer_in = arrived.reshape(fld * slots, width, lanes)
    joined = jnp.concatenate([query_weight, key_weight, value_weight, residual_weight], axis=2)
    weights = jnp.swapaxes(joined, 1, 2)
    fields = field_slot.shape[0]
    whole = fields == fld * slots
    if whole:
        order = field_slot[:, None] == jnp.arange(fields, dtype=jnp.int32)[None, :]
        weight_t = jnp.sum(jnp.where(order[:, None, :], out_weight[:, :, None], 0.0), axis=0)
    else:
        layer_in = jnp.take(layer_in, field_slot, axis=0)
        weight_t = jnp.transpose(out_weight)
    hidden, logits = interact(layer_in, weights, weight_t)
    if not whole:
        hidden = jnp.zeros((fld * slots, width, lanes), bf16).at[field_slot].set(hidden)
    placed = hidden.reshape(fld, slots, width, lanes)
    back = lax.all_to_all(placed, "fld", split_axis=0, concat_axis=0, tiled=True)
    interacted = jnp.transpose(back, (1, 0, 3, 2)).reshape(slots, fld * lanes, width)
    return interacted, logits


def solution(mesh):
    placed = (P("groups", "fld"), P(), P(("fld", "rep"), None), P(), P(), P(), P(), P())
    return jax.shard_map(
        per_device,
        mesh=mesh,
        in_specs=placed,
        out_specs=(P("fld", ("groups", "rep"), None), P("rep", ("groups", "fld"))),
        check_vma=False,
    )
```

```python
import functools
import math

import jax
import jax.numpy as jnp
from jax import lax
from jax.experimental import pallas as pl
from jax.experimental.pallas import tpu as pltpu
from jax.sharding import PartitionSpec as P

HEADS = 2
f32, bf16 = jnp.float32, jnp.bfloat16

MESH = pl.DeviceIdType.MESH


def greet(peers):
    barrier = pltpu.get_barrier_semaphore()
    for peer in peers:
        pl.semaphore_signal(barrier, inc=1, device_id=peer, device_id_type=MESH)
    return barrier


def interact_body(
    layers, heads, firsts, slots, fld, rep, found, wt, ow, out, logit,
    xs, q, k, v, skip, qt, att, mt, *links
):
    fields, width, lanes = xs.shape
    near = found.shape[1]
    size = width // heads
    scale = 1.0 / math.sqrt(size)
    gb, db = 4, 4
    if fld:
        staged, send, recv, keep, got, hop_send, hop_recv = links
        me = lax.axis_index("fld")
        half = lax.axis_index("rep")

        def peer(n, c):
            return lax.rem(me + n, fld), lax.rem(half + c, rep)

        def hop(n, c):
            to_fld, to_rep = peer(n, c)
            return pltpu.make_async_remote_copy(
                src_ref=found.at[to_rep * fld + to_fld], dst_ref=got.at[half * fld + me],
                send_sem=hop_send.at[n, c], recv_sem=hop_recv.at[n, c],
                device_id={"fld": to_fld, "rep": to_rep}, device_id_type=MESH,
            )
        others = [(n, c) for n in range(fld) for c in range(rep) if n or c]
        barrier = greet([{"fld": peer(n, c)[0], "rep": peer(n, c)[1]} for n, c in others])
        mine = pltpu.make_async_copy(found.at[half * fld + me], got.at[half * fld + me], keep.at[HEADS])
        mine.start()
        pl.semaphore_wait(barrier, len(others))
        for n, c in others:
            hop(n, c).start()

        def parcel(h, n):
            dest = lax.rem(me + 1 + n, fld)
            part = pl.ds(h * size, size)
            return pltpu.make_async_remote_copy(
                src_ref=staged.at[h, dest],
                dst_ref=out.at[:, part, pl.ds(pl.multiple_of(me * lanes, lanes), lanes)],
                send_sem=send.at[h, n], recv_sem=recv.at[h, n],
                device_id={"fld": dest}, device_id_type=MESH,
            )

    def project_one(l, f, value):
        p = jnp.dot(wt[l], value, preferred_element_type=f32)
        base = pl.multiple_of(f * width, width)
        q[pl.ds(base, width), :] = p[0:width].astype(bf16).astype(f32)
        k[pl.ds(base, width), :] = p[width:2 * width].astype(bf16).astype(f32)
        v[pl.ds(base, width), :] = p[2 * width:3 * width].astype(bf16).astype(f32)
        skip[pl.ds(base, width), :] = p[3 * width:4 * width]

    def turn(d, carry):
        qt[pl.ds(pl.multiple_of(d * fields, 8), fields), :] = q[pl.ds(d, fields, stride=width), :] * scale
        return carry

    def attend(h):
        def match(gi, top):
            acc = [jnp.zeros((fields, lanes), f32) for _ in range(gb)]
            for d in range(h * size, (h + 1) * size):
                qd = qt[d * fields:(d + 1) * fields, :]
                for j in range(gb):
                    row = k[pl.ds((gi * gb + j) * width + d, 1), :]
                    acc[j] = acc[j] + qd * row
            for j in range(gb):
                att[gi * gb + j] = acc[j]
                top = jnp.maximum(top, acc[j])
            return top
        top = lax.fori_loop(0, fields // gb, match, jnp.full((fields, lanes), -jnp.inf, f32))

        def expo(g, total):
            e = jnp.exp(att[g] - top)
            att[g] = e
            return total + e
        total = lax.fori_loop(0, fields, expo, jnp.zeros((fields, lanes), f32), unroll=4)
        inverse = 1.0 / total

        def norm(g, carry):
            att[g] = (att[g] * inverse).astype(bf16).astype(f32)
            return carry
        lax.fori_loop(0, fields, norm, 0, unroll=4)

        def mix(di, carry):
            acc = [jnp.zeros((fields, lanes), f32) for _ in range(db)]
            for g in range(fields):
                a = att[g]
                for j in range(db):
                    row = v[pl.ds(g * width + di * db + j, 1), :]
                    acc[j] = acc[j] + a * row
            for j in range(db):
                mt[pl.ds(pl.multiple_of((di * db + j) * fields, 8), fields), :] = acc[j]
            return carry
        lax.fori_loop(h * size // db, (h + 1) * size // db, mix, 0)

    def finish(f, h):
        m = mt[pl.ds(h * size * fields + f, size, stride=fields), :]
        s = skip[pl.ds(pl.multiple_of(f * width + h * size, size), size), :]
        return jnp.maximum(m + s, 0.0).astype(bf16)

    for l in range(layers):
        if l == 0:
            if fld:
                mine.wait()

                def arrive(n, carry):
                    p = lax.rem(me - n + fld, fld)
                    for s in range(slots):
                        terms = [got[r * fld + p, s - a] for r, a in enumerate(firsts) if 0 <= s - a < near]
                        project_one(0, p * slots + s, sum(terms[1:], terms[0]))
                    return carry

                def await_arrive(n, carry):
                    for c in range(rep):
                        hop(n, c).wait_recv()
                    return arrive(n, carry)
                for c in range(1, rep):
                    hop(0, c).wait_recv()
                arrive(0, 0)
                lax.fori_loop(1, fld, await_arrive, 0)
            else:
                def first_layer(f, carry):
                    project_one(0, f, found[f, 0])
                    return carry
                lax.fori_loop(0, fields, first_layer, 0, unroll=4)
        else:
            def next_layer(f, carry):
                project_one(l, f, xs[f])
                return carry
            lax.fori_loop(0, fields, next_layer, 0, unroll=4)
        lax.fori_loop(0, width, turn, 0, unroll=8)
        if l < layers - 1:
            for h in range(heads):
                attend(h)

            def close(f, carry):
                for h in range(heads):
                    xs[f, h * size:(h + 1) * size, :] = finish(f, h)
                return carry
            lax.fori_loop(0, fields, close, 0, unroll=4)
        else:
            total = jnp.zeros((size, lanes), f32)
            for h in range(heads):
                attend(h)
                for f in range(fields):
                    hid = finish(f, h)
                    if fld:
                        staged[h, f // slots, f % slots] = hid
                    else:
                        out[f, h * size:(h + 1) * size, :] = hid
                    total = total + hid.astype(f32) * ow[h * size:(h + 1) * size, f:f + 1]
                if fld:
                    for n in range(fld - 1):
                        parcel(h, n).start()
            logit[...] = jnp.sum(total, axis=0, keepdims=True)
    if fld:
        for h in range(heads):
            own = pltpu.make_async_copy(
                staged.at[h, me],
                out.at[:, pl.ds(h * size, size), pl.ds(pl.multiple_of(me * lanes, lanes), lanes)],
                keep.at[h],
            )
            own.start()
            own.wait()
        for h in range(heads):
            for n in range(fld - 1):
                parcel(h, n).wait()
        for n, c in others:
            hop(n, c).wait_send()


def interact(found, wt, ow, firsts, slots, fld, rep):
    fields = ow.shape[1]
    near, width, lanes = found.shape[1:]
    layers = wt.shape[0]
    flat = pltpu.VMEM((fields * width, lanes), f32)
    out_shape, links, extra = (fields, width, lanes), [], {}
    if fld:
        size = width // HEADS
        out_shape = (slots, width, fld * lanes)
        links = [
            pltpu.VMEM((HEADS, fld, slots, size, lanes), bf16),
            pltpu.SemaphoreType.DMA((HEADS, fld - 1)),
            pltpu.SemaphoreType.DMA((HEADS, fld - 1)),
            pltpu.SemaphoreType.DMA((HEADS + 1,)),
            pltpu.VMEM(found.shape, bf16),
            pltpu.SemaphoreType.DMA((fld, rep)),
            pltpu.SemaphoreType.DMA((fld, rep)),
        ]
        extra = dict(collective_id=0, has_side_effects=True)
    return pl.pallas_call(
        functools.partial(interact_body, layers, HEADS, firsts, slots, fld, rep),
        out_shape=(jax.ShapeDtypeStruct(out_shape, bf16), jax.ShapeDtypeStruct((1, lanes), f32)),
        in_specs=[pl.BlockSpec(memory_space=pltpu.VMEM)] * 3,
        out_specs=(pl.BlockSpec(memory_space=pltpu.VMEM),) * 2,
        scratch_shapes=[
            pltpu.VMEM((fields, width, lanes), bf16), flat, flat, flat, flat, flat,
            pltpu.VMEM((fields, fields, lanes), f32), flat,
        ] + links,
        compiler_params=pltpu.CompilerParams(vmem_limit_bytes=40 << 20, **extra),
    )(found, wt, ow)


def lookup_body(ready, starts, shifts, valid, table, out, held, sems):
    tiles, slots, width, lanes = out.shape
    piece = table.shape[1] // sems.shape[0]
    copies = [
        pltpu.make_async_copy(
            table.at[:, c * piece:(c + 1) * piece], held.at[:, c * piece:(c + 1) * piece], sems.at[c]
        )
        for c in range(sems.shape[0])
    ]
    for copy in copies:
        copy.start()
    lane = lax.broadcasted_iota(jnp.int32, (1, lanes), 1)
    done = 0
    for j in range(slots):
        while done < len(copies) and done * piece < ready[j]:
            copies[done].wait()
            done += 1

        def tile(t, carry):
            base = (j * tiles + t) * lanes
            acc = jnp.zeros((width, lanes), bf16)
            for i in range(lanes):
                start = pl.multiple_of(starts[base + i], 128)
                block = pltpu.roll(held[:, pl.ds(start, lanes)], shifts[base + i], 1)
                acc = jnp.where(lane == i, block, acc)
            keep = valid[j, pl.ds(t, 1), :] > 0
            out[t, j] = jnp.where(keep, acc, jnp.zeros_like(acc))
            return carry
        lax.fori_loop(0, tiles, tile, 0)
    for copy in copies[done:]:
        copy.wait()


def pieces(owned):
    return next(c for c in (5, 4, 3, 2, 1) if owned % (c * 128) == 0)


def lookup(starts, shifts, valid, table_t, ready):
    slots, tiles, lanes = valid.shape
    width, owned = table_t.shape
    return pl.pallas_call(
        functools.partial(lookup_body, ready),
        out_shape=jax.ShapeDtypeStruct((tiles, slots, width, lanes), bf16),
        in_specs=[
            pl.BlockSpec(memory_space=pltpu.SMEM),
            pl.BlockSpec(memory_space=pltpu.SMEM),
            pl.BlockSpec(memory_space=pltpu.VMEM),
            pl.BlockSpec(memory_space=pl.ANY),
        ],
        out_specs=pl.BlockSpec(memory_space=pltpu.VMEM),
        scratch_shapes=[
            pltpu.VMEM((width, owned), bf16),
            pltpu.SemaphoreType.DMA((pieces(owned),)),
        ],
        compiler_params=pltpu.CompilerParams(vmem_limit_bytes=48 << 20),
    )(starts, shifts, valid, table_t)


def per_device(
    feature_ids, field_slot, table, query_weight, key_weight, value_weight, residual_weight, out_weight
):
    examples, slots = feature_ids.shape
    owned, width = table.shape
    fld = lax.axis_size("fld")
    rep = lax.axis_size("rep")
    me = lax.axis_index("rep")
    rows_slot = owned * rep // slots
    lanes = examples // rep // fld
    firsts = [r * owned // rows_slot for r in range(rep)]
    lasts = [-(-(r + 1) * owned // rows_slot) for r in range(rep)]
    near = max(b - a for a, b in zip(firsts, lasts))
    firsts = [min(a, slots - near) for a in firsts]
    ready = [
        max(min(owned, (a + j + 1) * rows_slot - r * owned) for r, a in enumerate(firsts))
        for j in range(near)
    ]
    first = sum((me == r) * a for r, a in enumerate(firsts)).astype(jnp.int32)
    near_ids = lax.dynamic_slice_in_dim(jnp.transpose(feature_ids), first, near, 0)
    offset = (first + jnp.arange(near, dtype=jnp.int32)) * rows_slot - me * owned
    rows = near_ids + offset[:, None]
    valid = ((rows >= 0) & (rows < owned)).astype(jnp.int32)
    rows = jnp.clip(rows, 0, owned - 1)
    starts = (rows >> 7) << 7
    shifts = (jnp.arange(examples, dtype=jnp.int32)[None, :] - rows) & 127
    found = lookup(
        starts.reshape(-1), shifts.reshape(-1), valid.reshape(near, -1, lanes), jnp.transpose(table), ready
    )
    joined = jnp.concatenate([query_weight, key_weight, value_weight, residual_weight], axis=2)
    weights = jnp.swapaxes(joined, 1, 2)
    fields = field_slot.shape[0]
    if fields == fld * slots:
        order = field_slot[:, None] == jnp.arange(fields, dtype=jnp.int32)[None, :]
        weight_t = jnp.sum(jnp.where(order[:, None, :], out_weight[:, :, None], 0.0), axis=0)
        back, logits = interact(found, weights, weight_t, firsts, slots, fld, rep)
        return jnp.swapaxes(back, 1, 2), logits
    found = found.reshape(rep, fld, near, width, lanes)
    looked = jnp.zeros((fld, slots, width, lanes), bf16)
    looked = lax.dynamic_update_slice_in_dim(looked, lax.dynamic_index_in_dim(found, me, 0, False), first, 1)
    for step in range(1, rep):
        route = [(r, (r + step) % rep) for r in range(rep)]
        other = lax.ppermute(lax.dynamic_index_in_dim(found, (me + step) % rep, 0, False), "rep", route)
        source = (me - step) % rep
        start = sum((source == r) * a for r, a in enumerate(firsts)).astype(jnp.int32)
        old = lax.dynamic_slice_in_dim(looked, start, near, 1)
        looked = lax.dynamic_update_slice_in_dim(looked, old + other, start, 1)
    arrived = lax.all_to_all(looked, "fld", split_axis=0, concat_axis=0, tiled=True)
    layer_in = jnp.take(arrived.reshape(fld * slots, width, lanes), field_slot, axis=0)
    weight_t = jnp.transpose(out_weight)
    hidden, logits = interact(layer_in[:, None], weights, weight_t, [0], 1, 0, 0)
    hidden = jnp.zeros((fld * slots, width, lanes), bf16).at[field_slot].set(hidden)
    placed = hidden.reshape(fld, slots, width, lanes)
    back = lax.all_to_all(placed, "fld", split_axis=0, concat_axis=0, tiled=True)
    interacted = jnp.transpose(back, (1, 0, 3, 2)).reshape(slots, fld * lanes, width)
    return interacted, logits


def solution(mesh):
    placed = (P("groups", "fld"), P(), P(("fld", "rep"), None), P(), P(), P(), P(), P())
    return jax.shard_map(
        per_device,
        mesh=mesh,
        in_specs=placed,
        out_specs=(P("fld", ("groups", "rep"), None), P("rep", ("groups", "fld"))),
        check_vma=False,
    )
```

```python
import functools
import math

import jax
import jax.numpy as jnp
from jax import lax
from jax.experimental import pallas as pl
from jax.experimental.pallas import tpu as pltpu
from jax.sharding import PartitionSpec as P

HEADS = 2
f32, bf16 = jnp.float32, jnp.bfloat16

MESH = pl.DeviceIdType.MESH


def greet(peers):
    barrier = pltpu.get_barrier_semaphore()
    for peer in peers:
        pl.semaphore_signal(barrier, inc=1, device_id=peer, device_id_type=MESH)
    return barrier


def interact_body(
    layers, heads, firsts, slots, fld, rep, found, wq, wk, wv, ws, ow, out, logit,
    wt, xs, q, k, v, skip, qt, att, mt, *links
):
    fields, width, lanes = xs.shape
    near = found.shape[1]
    size = width // heads
    scale = 1.0 / math.sqrt(size)
    gb, db = 4, 4
    if fld:
        staged, send, recv, keep, got, hop_send, hop_recv = links
        me = lax.axis_index("fld")
        half = lax.axis_index("rep")

        def peer(n, c):
            return lax.rem(me + n, fld), lax.rem(half + c, rep)

        def hop(n, c):
            to_fld, to_rep = peer(n, c)
            return pltpu.make_async_remote_copy(
                src_ref=found.at[to_rep * fld + to_fld], dst_ref=got.at[half * fld + me],
                send_sem=hop_send.at[n, c], recv_sem=hop_recv.at[n, c],
                device_id={"fld": to_fld, "rep": to_rep}, device_id_type=MESH,
            )
        others = [(n, c) for n in range(fld) for c in range(rep) if n or c]
        barrier = greet([{"fld": peer(n, c)[0], "rep": peer(n, c)[1]} for n, c in others])
        mine = pltpu.make_async_copy(found.at[half * fld + me], got.at[half * fld + me], keep.at[HEADS])
        mine.start()
        pl.semaphore_wait(barrier, len(others))
        for n, c in others:
            hop(n, c).start()

        def parcel(h, n):
            dest = lax.rem(me + 1 + n, fld)
            part = pl.ds(h * size, size)
            return pltpu.make_async_remote_copy(
                src_ref=staged.at[h, dest],
                dst_ref=out.at[:, part, pl.ds(pl.multiple_of(me * lanes, lanes), lanes)],
                send_sem=send.at[h, n], recv_sem=recv.at[h, n],
                device_id={"fld": dest}, device_id_type=MESH,
            )

    for l in range(layers):
        for n, w in enumerate((wq, wk, wv, ws)):
            wt[l, n * width:(n + 1) * width, :] = jnp.transpose(w[l].astype(f32)).astype(bf16)

    def project_one(l, f, value):
        p = jnp.dot(wt[l], value, preferred_element_type=f32)
        base = pl.multiple_of(f * width, width)
        q[pl.ds(base, width), :] = p[0:width].astype(bf16).astype(f32)
        k[pl.ds(base, width), :] = p[width:2 * width].astype(bf16).astype(f32)
        v[pl.ds(base, width), :] = p[2 * width:3 * width].astype(bf16).astype(f32)
        skip[pl.ds(base, width), :] = p[3 * width:4 * width]

    def turn(d, carry):
        qt[pl.ds(pl.multiple_of(d * fields, 8), fields), :] = q[pl.ds(d, fields, stride=width), :] * scale
        return carry

    def attend(h):
        def match(gi, top):
            acc = [jnp.zeros((fields, lanes), f32) for _ in range(gb)]
            for d in range(h * size, (h + 1) * size):
                qd = qt[d * fields:(d + 1) * fields, :]
                for j in range(gb):
                    row = k[pl.ds((gi * gb + j) * width + d, 1), :]
                    acc[j] = acc[j] + qd * row
            for j in range(gb):
                att[gi * gb + j] = acc[j]
                top = jnp.maximum(top, acc[j])
            return top
        top = lax.fori_loop(0, fields // gb, match, jnp.full((fields, lanes), -jnp.inf, f32))

        def expo(g, total):
            e = jnp.exp(att[g] - top)
            att[g] = e
            return total + e
        total = lax.fori_loop(0, fields, expo, jnp.zeros((fields, lanes), f32), unroll=4)
        inverse = 1.0 / total

        def norm(g, carry):
            att[g] = (att[g] * inverse).astype(bf16).astype(f32)
            return carry
        lax.fori_loop(0, fields, norm, 0, unroll=4)

        def mix(di, carry):
            acc = [jnp.zeros((fields, lanes), f32) for _ in range(db)]
            for g in range(fields):
                a = att[g]
                for j in range(db):
                    row = v[pl.ds(g * width + di * db + j, 1), :]
                    acc[j] = acc[j] + a * row
            for j in range(db):
                mt[pl.ds(pl.multiple_of((di * db + j) * fields, 8), fields), :] = acc[j]
            return carry
        lax.fori_loop(h * size // db, (h + 1) * size // db, mix, 0)

    def finish(f, h):
        m = mt[pl.ds(h * size * fields + f, size, stride=fields), :]
        s = skip[pl.ds(pl.multiple_of(f * width + h * size, size), size), :]
        return jnp.maximum(m + s, 0.0).astype(bf16)

    for l in range(layers):
        if l == 0:
            if fld:
                mine.wait()

                def arrive(n, carry):
                    p = lax.rem(me - n + fld, fld)
                    for s in range(slots):
                        terms = [got[r * fld + p, s - a] for r, a in enumerate(firsts) if 0 <= s - a < near]
                        project_one(0, p * slots + s, sum(terms[1:], terms[0]))
                    return carry

                def await_arrive(n, carry):
                    for c in range(rep):
                        hop(n, c).wait_recv()
                    return arrive(n, carry)
                for c in range(1, rep):
                    hop(0, c).wait_recv()
                arrive(0, 0)
                lax.fori_loop(1, fld, await_arrive, 0)
            else:
                def first_layer(f, carry):
                    project_one(0, f, found[f, 0])
                    return carry
                lax.fori_loop(0, fields, first_layer, 0, unroll=4)
        else:
            def next_layer(f, carry):
                project_one(l, f, xs[f])
                return carry
            lax.fori_loop(0, fields, next_layer, 0, unroll=4)
        lax.fori_loop(0, width, turn, 0, unroll=8)
        if l < layers - 1:
            for h in range(heads):
                attend(h)

            def close(f, carry):
                for h in range(heads):
                    xs[f, h * size:(h + 1) * size, :] = finish(f, h)
                return carry
            lax.fori_loop(0, fields, close, 0, unroll=4)
        else:
            total = jnp.zeros((size, lanes), f32)
            for h in range(heads):
                attend(h)
                for f in range(fields):
                    hid = finish(f, h)
                    if fld:
                        staged[h, f // slots, f % slots] = hid
                    else:
                        out[f, h * size:(h + 1) * size, :] = hid
                    total = total + hid.astype(f32) * ow[h * size:(h + 1) * size, f:f + 1]
                if fld:
                    for n in range(fld - 1):
                        parcel(h, n).start()
            logit[...] = jnp.sum(total, axis=0, keepdims=True)
    if fld:
        for h in range(heads):
            own = pltpu.make_async_copy(
                staged.at[h, me],
                out.at[:, pl.ds(h * size, size), pl.ds(pl.multiple_of(me * lanes, lanes), lanes)],
                keep.at[h],
            )
            own.start()
            own.wait()
        for h in range(heads):
            for n in range(fld - 1):
                parcel(h, n).wait()
        for n, c in others:
            hop(n, c).wait_send()


def interact(found, weights, ow, firsts, slots, fld, rep):
    fields = ow.shape[1]
    near, width, lanes = found.shape[1:]
    layers = weights[0].shape[0]
    flat = pltpu.VMEM((fields * width, lanes), f32)
    out_shape, links, extra = (fields, width, lanes), [], {}
    if fld:
        size = width // HEADS
        out_shape = (slots, width, fld * lanes)
        links = [
            pltpu.VMEM((HEADS, fld, slots, size, lanes), bf16),
            pltpu.SemaphoreType.DMA((HEADS, fld - 1)),
            pltpu.SemaphoreType.DMA((HEADS, fld - 1)),
            pltpu.SemaphoreType.DMA((HEADS + 1,)),
            pltpu.VMEM(found.shape, bf16),
            pltpu.SemaphoreType.DMA((fld, rep)),
            pltpu.SemaphoreType.DMA((fld, rep)),
        ]
        extra = dict(collective_id=0, has_side_effects=True)
    return pl.pallas_call(
        functools.partial(interact_body, layers, HEADS, firsts, slots, fld, rep),
        out_shape=(jax.ShapeDtypeStruct(out_shape, bf16), jax.ShapeDtypeStruct((1, lanes), f32)),
        in_specs=[pl.BlockSpec(memory_space=pltpu.VMEM)] * 6,
        out_specs=(pl.BlockSpec(memory_space=pltpu.VMEM),) * 2,
        scratch_shapes=[
            pltpu.VMEM((layers, 4 * width, width), bf16),
            pltpu.VMEM((fields, width, lanes), bf16), flat, flat, flat, flat, flat,
            pltpu.VMEM((fields, fields, lanes), f32), flat,
        ] + links,
        compiler_params=pltpu.CompilerParams(vmem_limit_bytes=40 << 20, **extra),
    )(found, *weights, ow)


def lookup_body(ready, starts, shifts, valid, table, out, held, sems):
    tiles, slots, width, lanes = out.shape
    piece = table.shape[1] // sems.shape[0]
    copies = [
        pltpu.make_async_copy(
            table.at[:, c * piece:(c + 1) * piece], held.at[:, c * piece:(c + 1) * piece], sems.at[c]
        )
        for c in range(sems.shape[0])
    ]
    for copy in copies:
        copy.start()
    lane = lax.broadcasted_iota(jnp.int32, (1, lanes), 1)
    done = 0
    for j in range(slots):
        while done < len(copies) and done * piece < ready[j]:
            copies[done].wait()
            done += 1

        def tile(t, carry):
            base = (j * tiles + t) * lanes
            acc = jnp.zeros((width, lanes), bf16)
            for i in range(lanes):
                start = pl.multiple_of(starts[base + i], 128)
                block = pltpu.roll(held[:, pl.ds(start, lanes)], shifts[base + i], 1)
                acc = jnp.where(lane == i, block, acc)
            keep = valid[j, pl.ds(t, 1), :] > 0
            out[t, j] = jnp.where(keep, acc, jnp.zeros_like(acc))
            return carry
        lax.fori_loop(0, tiles, tile, 0)
    for copy in copies[done:]:
        copy.wait()


def pieces(owned):
    return next(c for c in (5, 4, 3, 2, 1) if owned % (c * 128) == 0)


def lookup(starts, shifts, valid, table_t, ready):
    slots, tiles, lanes = valid.shape
    width, owned = table_t.shape
    return pl.pallas_call(
        functools.partial(lookup_body, ready),
        out_shape=jax.ShapeDtypeStruct((tiles, slots, width, lanes), bf16),
        in_specs=[
            pl.BlockSpec(memory_space=pltpu.SMEM),
            pl.BlockSpec(memory_space=pltpu.SMEM),
            pl.BlockSpec(memory_space=pltpu.VMEM),
            pl.BlockSpec(memory_space=pl.ANY),
        ],
        out_specs=pl.BlockSpec(memory_space=pltpu.VMEM),
        scratch_shapes=[
            pltpu.VMEM((width, owned), bf16),
            pltpu.SemaphoreType.DMA((pieces(owned),)),
        ],
        compiler_params=pltpu.CompilerParams(vmem_limit_bytes=48 << 20),
    )(starts, shifts, valid, table_t)


def per_device(
    feature_ids, field_slot, table, query_weight, key_weight, value_weight, residual_weight, out_weight
):
    examples, slots = feature_ids.shape
    owned, width = table.shape
    fld = lax.axis_size("fld")
    rep = lax.axis_size("rep")
    me = lax.axis_index("rep")
    rows_slot = owned * rep // slots
    lanes = examples // rep // fld
    firsts = [r * owned // rows_slot for r in range(rep)]
    lasts = [-(-(r + 1) * owned // rows_slot) for r in range(rep)]
    near = max(b - a for a, b in zip(firsts, lasts))
    firsts = [min(a, slots - near) for a in firsts]
    ready = [
        max(min(owned, (a + j + 1) * rows_slot - r * owned) for r, a in enumerate(firsts))
        for j in range(near)
    ]
    first = sum((me == r) * a for r, a in enumerate(firsts)).astype(jnp.int32)
    near_ids = lax.dynamic_slice_in_dim(jnp.transpose(feature_ids), first, near, 0)
    offset = (first + jnp.arange(near, dtype=jnp.int32)) * rows_slot - me * owned
    rows = near_ids + offset[:, None]
    valid = ((rows >= 0) & (rows < owned)).astype(jnp.int32)
    rows = jnp.clip(rows, 0, owned - 1)
    starts = (rows >> 7) << 7
    shifts = (jnp.arange(examples, dtype=jnp.int32)[None, :] - rows) & 127
    found = lookup(
        starts.reshape(-1), shifts.reshape(-1), valid.reshape(near, -1, lanes), jnp.transpose(table), ready
    )
    weights = (query_weight, key_weight, value_weight, residual_weight)
    fields = field_slot.shape[0]
    if fields == fld * slots:
        order = field_slot[:, None] == jnp.arange(fields, dtype=jnp.int32)[None, :]
        weight_t = jnp.sum(jnp.where(order[:, None, :], out_weight[:, :, None], 0.0), axis=0)
        back, logits = interact(found, weights, weight_t, firsts, slots, fld, rep)
        return jnp.swapaxes(back, 1, 2), logits
    found = found.reshape(rep, fld, near, width, lanes)
    looked = jnp.zeros((fld, slots, width, lanes), bf16)
    looked = lax.dynamic_update_slice_in_dim(looked, lax.dynamic_index_in_dim(found, me, 0, False), first, 1)
    for step in range(1, rep):
        route = [(r, (r + step) % rep) for r in range(rep)]
        other = lax.ppermute(lax.dynamic_index_in_dim(found, (me + step) % rep, 0, False), "rep", route)
        source = (me - step) % rep
        start = sum((source == r) * a for r, a in enumerate(firsts)).astype(jnp.int32)
        old = lax.dynamic_slice_in_dim(looked, start, near, 1)
        looked = lax.dynamic_update_slice_in_dim(looked, old + other, start, 1)
    arrived = lax.all_to_all(looked, "fld", split_axis=0, concat_axis=0, tiled=True)
    layer_in = jnp.take(arrived.reshape(fld * slots, width, lanes), field_slot, axis=0)
    weight_t = jnp.transpose(out_weight)
    hidden, logits = interact(layer_in[:, None], weights, weight_t, [0], 1, 0, 0)
    hidden = jnp.zeros((fld * slots, width, lanes), bf16).at[field_slot].set(hidden)
    placed = hidden.reshape(fld, slots, width, lanes)
    back = lax.all_to_all(placed, "fld", split_axis=0, concat_axis=0, tiled=True)
    interacted = jnp.transpose(back, (1, 0, 3, 2)).reshape(slots, fld * lanes, width)
    return interacted, logits


def solution(mesh):
    placed = (P("groups", "fld"), P(), P(("fld", "rep"), None), P(), P(), P(), P(), P())
    return jax.shard_map(
        per_device,
        mesh=mesh,
        in_specs=placed,
        out_specs=(P("fld", ("groups", "rep"), None), P("rep", ("groups", "fld"))),
        check_vma=False,
    )
```
